32 devices in a mesh: wide: 8 (over z, x), narrow: 4 (over y, core).
Axes of the slice: x: 2, y: 2, z: 4, core: 2. Of those that a mesh axis runs over, the one named last changes fastest.
Arguments:
- mass_field: bfloat16 [64, 1024, 1024], P('wide', 'narrow'), may hold values from -6 to 6
- heat_field: bfloat16 [64, 1024, 1024], P('wide', 'narrow'), may hold values from -6 to 6
- segment_lookup_pick: int32 [64, 1024], P('wide', 'narrow'), may hold values from 0 to 7
- mapping_kernel_means: float32 [8, 8], replicated, may hold values from -2 to 2
- mapping_kernel_widths: float32 [8, 8], replicated, may hold values from 0.5 to 3
- mapping_kernel_heights: float32 [8, 8], replicated, may hold values from 0.05 to 2
- tint_scale_shift: float32 [8, 6], replicated, may hold values from -6 to 6
Outputs:
- image: float32 [4, 32, 8, 4, 1024], P('narrow', None, 'wide')
The draws below stay inside these ranges and needn't reach their ends.
All inputs are finite; a program needn't handle non-finite values.
Results may differ from the reference program's by a relative error of at most 0.0003.
Values may be sent and summed in bfloat16 or wider, within the bound.
No kernel may reach another device: no remote copies, remote signals or barrier semaphores. Data moves between devices by JAX's collectives and lax.ppermute only.
A program may use at most 128 MiB of HBM per device.

```python
import math
import jax
import jax.numpy as jnp
from jax import lax

PIXEL_ACROSS = 1024
ROWS_DEV = 256
NTF = 8
BUMPS = 8
SLAB_THICKNESS = 64
PIXEL_DOWN = 1024
N_WIDE = 8
N_NARROW = 4


def plant(array, rng, low, top_value):
    shape = array.shape
    index_at = [jax.random.randint(jax.random.fold_in(rng, axis), (), 0, shape[axis]) for axis in range(len(shape))]
    array = array.at[tuple(index_at)].set(low)
    longest = shape.index(max(shape))
    index_at[longest] = (index_at[longest] + 1) % shape[longest]
    return array.at[tuple(index_at)].set(top_value)


def levels(stream_key, extent, cuts, least, top_value):
    def one(dim, blocks):
        steps = jax.random.uniform(jax.random.fold_in(jax.random.fold_in(stream_key, 6), dim), (blocks,), jnp.float32, least / len(cuts), top_value / len(cuts))
        return jnp.repeat(jnp.exp(steps), extent[dim] // blocks).reshape((-1,) + (1,) * (len(extent) - dim - 1))

    factor_of = one(*cuts[0])
    for cut in cuts[1:]:
        factor_of = factor_of * one(*cut)
    return factor_of


def gaussian(key, dims, deviation, most, cuts=(), kind=jnp.bfloat16):
    gain = levels(key, dims, cuts, -0.22, 0.18) if cuts else 1.0
    entries = jax.random.normal(key, dims, jnp.float32) * deviation * gain
    return jnp.minimum(jnp.maximum(entries, -most), most).astype(kind)


def setup_inputs(seed: int = 0) -> dict:
    seeds = jax.random.split(jax.random.key(seed), 8)
    mass_field = gaussian(seeds[0], (SLAB_THICKNESS, PIXEL_DOWN, PIXEL_ACROSS), 1.0, 6.0, ((0, 8), (1, 4)))
    heat_field = gaussian(seeds[1], (SLAB_THICKNESS, PIXEL_DOWN, PIXEL_ACROSS), 1.0, 6.0, ((0, 8), (1, 4)))
    segment_lookup_pick = plant(jax.random.randint(seeds[2], (SLAB_THICKNESS, PIXEL_DOWN), 0, NTF), jax.random.fold_in(seeds[2], 1), 0, NTF - 1).astype(jnp.int32)
    mapping_kernel_means = jnp.clip(jax.random.uniform(seeds[3], (NTF, BUMPS), jnp.float32, -2.0, 2.0), -2.0, 2.0)
    mapping_kernel_widths = jnp.clip(jnp.exp(jax.random.uniform(seeds[4], (NTF, BUMPS), jnp.float32, math.log(0.5), math.log(3.0))), 0.5, 3.0)
    mapping_kernel_heights = jnp.clip(jnp.exp(jax.random.uniform(seeds[5], (NTF, BUMPS), jnp.float32, math.log(0.05), math.log(2.0))), 0.05, 2.0)
    tint_scale_shift = gaussian(seeds[6], (NTF, 6), 1.5, 6.0, (), jnp.float32)
    return {"mass_field": mass_field, "heat_field": heat_field, "segment_lookup_pick": segment_lookup_pick, "mapping_kernel_means": mapping_kernel_means, "mapping_kernel_widths": mapping_kernel_widths, "mapping_kernel_heights": mapping_kernel_heights, "tint_scale_shift": tint_scale_shift}


step_length = 0.003
light_depth = 0.64
light_rows = 0.6
light_cols = 0.48

def line_tables(picks, mapping_kernel_means, mapping_kernel_widths, mapping_kernel_heights, tint_scale_shift):
    onehot = (picks[..., None] == jnp.arange(mapping_kernel_means.shape[0], dtype=jnp.int32)).astype(jnp.float32)
    highest = lax.Precision.HIGHEST
    kernel_means = jnp.einsum('...t,tg->...g', onehot, mapping_kernel_means, precision=highest)
    kernel_widths = jnp.einsum('...t,tg->...g', onehot, mapping_kernel_widths, precision=highest)
    kernel_heights = jnp.einsum('...t,tg->...g', onehot, mapping_kernel_heights, precision=highest)
    tint_values = jnp.einsum('...t,tg->...g', onehot, tint_scale_shift, precision=highest)
    return (kernel_means, kernel_widths, kernel_heights, tint_values)

def lit_slice(gathered_layers, heat_slice, kernel_means, kernel_widths, kernel_heights, tint_values):
    middle = gathered_layers[1, 1:-1]
    grad_depth = (gathered_layers[2, 1:-1] - gathered_layers[0, 1:-1]) * 0.5
    grad_rows = (gathered_layers[1, 2:] - gathered_layers[1, :-2]) * 0.5
    widened = jnp.pad(middle, ((0, 0), (1, 1)))
    grad_cols = (widened[:, 2:] - widened[:, :-2]) * 0.5
    extinction = jnp.zeros_like(middle)
    for bump in range(kernel_means.shape[1]):
        offset = kernel_widths[:, bump:bump + 1] * (middle - kernel_means[:, bump:bump + 1])
        extinction = extinction + kernel_heights[:, bump:bump + 1] * jnp.exp(-offset * offset)
    coverage = 1.0 - jnp.exp(-step_length * extinction)
    facing = grad_depth * light_depth + grad_rows * light_rows + grad_cols * light_cols
    norm_sq = grad_depth * grad_depth + grad_rows * grad_rows + grad_cols * grad_cols + 1.0
    lighting = 0.3 + 0.7 * jnp.abs(facing) * lax.rsqrt(norm_sq)
    blend_factor = coverage * lighting
    hued_samples = [jax.nn.sigmoid(heat_slice * tint_values[:, hue_component:hue_component + 1] + tint_values[:, 3 + hue_component:4 + hue_component]) * blend_factor for hue_component in range(3)]
    return (hued_samples, coverage)

def reference(mass_field, heat_field, segment_lookup_pick, mapping_kernel_means, mapping_kernel_widths, mapping_kernel_heights, tint_scale_shift):
    depth_total = mass_field.shape[0]
    row_total = mass_field.shape[1]
    col_total = mass_field.shape[2]

    def advance(carry, slice_number):
        accum, transmit = carry
        center_plane = lax.dynamic_index_in_dim(mass_field, slice_number, 0, keepdims=False).astype(jnp.float32)
        before = lax.dynamic_index_in_dim(mass_field, jnp.maximum(slice_number - 1, 0), 0, keepdims=False).astype(jnp.float32)
        before = jnp.where(slice_number > 0, before, jnp.zeros_like(before))
        after = lax.dynamic_index_in_dim(mass_field, jnp.minimum(slice_number + 1, depth_total - 1), 0, keepdims=False).astype(jnp.float32)
        after = jnp.where(slice_number < depth_total - 1, after, jnp.zeros_like(after))
        gathered_layers = jnp.pad(jnp.stack([before, center_plane, after]), ((0, 0), (1, 1), (0, 0)))
        heat_slice = lax.dynamic_index_in_dim(heat_field, slice_number, 0, keepdims=False).astype(jnp.float32)
        picks = lax.dynamic_index_in_dim(segment_lookup_pick, slice_number, 0, keepdims=False)
        kernel_means, kernel_widths, kernel_heights, tint_values = line_tables(picks, mapping_kernel_means, mapping_kernel_widths, mapping_kernel_heights, tint_scale_shift)
        hued_samples, coverage = lit_slice(gathered_layers, heat_slice, kernel_means, kernel_widths, kernel_heights, tint_values)
        accum = accum + transmit[:, None, :] * jnp.stack(hued_samples, axis=1)
        transmit = transmit * (1.0 - coverage)
        return ((accum, transmit), None)
    start = (jnp.zeros((row_total, 3, col_total), jnp.float32), jnp.ones((row_total, col_total), jnp.float32))
    (accum, transmit), ignored = lax.scan(advance, start, jnp.arange(depth_total, dtype=jnp.int32))
    picture = jnp.concatenate([accum, (1.0 - transmit)[:, None, :]], axis=1)
    return picture.reshape(N_NARROW, ROWS_DEV // N_WIDE, N_WIDE, 4, col_total)
```

```python
import functools
import math

import jax
import jax.numpy as jnp
from jax import lax
from jax.experimental import pallas as pl
from jax.experimental.pallas import tpu as pltpu
from jax.sharding import PartitionSpec as P

STEP = 0.003
LOG2E = math.log2(math.e)
SHADE = 0.7
L_DEPTH, L_ROWS, L_COLS = 0.64 * SHADE, 0.6 * SHADE, 0.48 * SHADE
K_EXT = -STEP * LOG2E

OCTAVES = 22.0
SCALE = 65534.0 / OCTAVES
TOP_COLOR = 0.0
TOP_EXT = 9.0

PARTS = 2
ROW_BLOCK = 32
COLS_STEP = 256
GROUP = 16
BLOCKS = 13
WIDTH = BLOCKS * GROUP
UNROLL = 2


def encode(value, top):
    code = jnp.log2(value) * SCALE + ((OCTAVES - top) * SCALE + 1.5)
    return (jnp.maximum(code, 0.0).astype(jnp.int32) - 32768).astype(jnp.int16)


def decode(code, top):
    code = code.astype(jnp.int32).astype(jnp.float32)
    value = jnp.exp2(code * (1.0 / SCALE) + (top - OCTAVES + 32767.0 / SCALE))
    return jnp.where(code > -32768.0, value, 0.0)


def tops(channel):
    return TOP_COLOR if channel < 3 else TOP_EXT


def shade_kernel(mode, first, last, *refs):
    mass, above, below, outer_up, outer_down, heat, lanes, picks, table, tint, row_diff = refs[:11]
    refs = refs[11:]
    low = high = inner = send = partial = None
    if mode != "inner":
        low, high, *refs = refs
    if mode == "outer":
        inner, *refs = refs
    result, a_s, tint_s, pick_s, edge_s, *refs = refs
    if mode == "inner":
        partial = result
    else:
        send = result
        (acc_s,) = refs
    step = pl.program_id(0)
    depth, rows, cols = mass.shape
    tables, bumps, _ = table.shape
    groups = rows // GROUP
    diagonal = lax.broadcasted_iota(jnp.int32, (GROUP, WIDTH), 1) % GROUP == (
        lax.broadcasted_iota(jnp.int32, (GROUP, WIDTH), 0)
    )
    lane = lax.broadcasted_iota(jnp.int32, (GROUP, 128), 1)
    ones = jnp.ones((GROUP, COLS_STEP), jnp.bfloat16)
    parts = COLS_STEP // 128
    layers = {"full": range(depth), "inner": range(1, depth - 1), "outer": (0, depth - 1)}[mode]

    @pl.when(step == 0)
    def _():
        pick_s[...] = picks[...].T

    def edges(z, _):
        edge_s[0, z] = above[z]
        edge_s[1, z] = below[z]
        return 0

    lax.fori_loop(0, depth, edges, 0)
    if first:
        @pl.when(step == 0)
        def _():
            for z in range(depth):
                edge_s[0, z] = jnp.broadcast_to(outer_up[z], edge_s.shape[2:])
    if last:
        @pl.when(step == pl.num_programs(0) - 1)
        def _():
            for z in range(depth):
                edge_s[1, z] = jnp.broadcast_to(outer_down[z], edge_s.shape[2:])

    for group in range(groups):
        at = GROUP * group

        def spread(z, at=at, group=group):
            chosen = jnp.broadcast_to(lanes[z, group], (bumps, WIDTH))
            line = table[0]
            for t in range(1, tables):
                line = jnp.where(chosen == t, table[t], line)
            for k in range(bumps):
                wide = jnp.broadcast_to(line[k : k + 1], (GROUP, WIDTH))
                a_s[z, GROUP * k : GROUP * (k + 1)] = jnp.where(diagonal, wide, 0.0).astype(
                    jnp.bfloat16
                )
            a_s[z, GROUP * bumps :] = row_diff[...]

        def stain(z, at=at):
            spot = pl.ds(pl.multiple_of(step * rows, rows) + at, GROUP)
            chosen = jnp.broadcast_to(pick_s[spot, z : z + 1], (GROUP, 128))
            line = jnp.broadcast_to(tint[0:1], (GROUP, 128))
            for t in range(1, tables):
                line = jnp.where(chosen == t, tint[t : t + 1], line)
            for k in range(6):
                tint_s[z, k] = jnp.broadcast_to(line[:, k : k + 1], (GROUP, 128))

        if mode == "outer":
            for z in layers:
                spread(z)
        else:
            lax.fori_loop(layers[0], layers[-1] + 1, lambda z, _: spread(z) or 0, 0)
        for z in layers:
            stain(z)

        def columns(block, _, at=at, group=group):
            base = pl.multiple_of(COLS_STEP * block, COLS_STEP)
            w = pl.ds(base, COLS_STEP)
            before = pl.ds(pl.multiple_of(jnp.maximum(base - 128, 0), 128), 128)
            beyond = pl.ds(
                pl.multiple_of(jnp.minimum(base + COLS_STEP, cols - 128), 128), 128
            )

            def plane(z):
                if z < 0:
                    return low[0, at : at + GROUP, w]
                if z == depth:
                    return high[0, at : at + GROUP, w]
                return mass[z, at : at + GROUP, w]

            def split(value):
                return [value[:, 128 * j : 128 * (j + 1)] for j in range(parts)]

            def tile(z, part, outside):
                value = mass[z, at : at + GROUP, part].astype(jnp.float32)
                return jnp.where(outside, 0.0, value)

            one = jnp.ones((GROUP, 128), jnp.float32)
            zero = jnp.zeros((GROUP, 128), jnp.float32)
            trans = [one] * parts
            total = [zero] * parts
            weight = [zero] * parts
            tinted = [[zero] * parts for _ in range(3)]
            for z in layers:
                if mode == "outer" and z:
                    for j in range(parts):
                        v = pl.ds(pl.multiple_of(base + 128 * j, 128), 128)
                        for c in range(3):
                            within = inner[c, at : at + GROUP, v]
                            tinted[c][j] = tinted[c][j] + (2.0 * trans[j]) * within
                        total[j] = total[j] + inner[3, at : at + GROUP, v]
                        trans[j] = jnp.exp2(total[j] * K_EXT)
                previous = plane(z - 1).astype(jnp.float32)
                current16 = plane(z)
                current = current16.astype(jnp.float32)
                following = plane(z + 1).astype(jnp.float32)
                square = current * current
                high16 = square.astype(jnp.bfloat16)
                low16 = (square - high16.astype(jnp.float32)).astype(jnp.bfloat16)
                warm = split(heat[z, at : at + GROUP, w].astype(jnp.float32))
                up16 = edge_s[0, z, :, w] if group == 0 else mass[z, at - GROUP : at, w]
                down16 = (
                    edge_s[1, z, :, w]
                    if group == groups - 1
                    else mass[z, at + GROUP : at + 2 * GROUP, w]
                )
                stacked = jnp.concatenate(
                    [high16] * 3 + [low16] * 2 + [current16] * 3 + [ones] * 3 + [up16, down16],
                    axis=0,
                )
                product = jnp.dot(a_s[z], stacked, preferred_element_type=jnp.float32)
                d_depth = split(following - previous)
                mids = [
                    tile(z, before, block == 0),
                    *split(current),
                    tile(z, beyond, block == cols // COLS_STEP - 1),
                ]
                to_right = [pltpu.roll(v, 1, 1) for v in mids[:-1]]
                to_left = [pltpu.roll(v, 127, 1) for v in mids[1:]]
                for j in range(parts):
                    def out(k):
                        return product[GROUP * k : GROUP * (k + 1), 128 * j : 128 * (j + 1)]

                    ext = jnp.exp2(out(0))
                    for g in range(1, bumps):
                        ext = ext + jnp.exp2(out(g))
                    d_row = out(bumps)
                    left = jnp.where(lane == 0, to_right[j], to_right[j + 1])
                    right = jnp.where(lane == 127, to_left[j + 1], to_left[j])
                    d_col = right - left
                    facing = d_row * L_ROWS + d_col * L_COLS + d_depth[j] * L_DEPTH
                    norm = d_row * d_row + d_col * d_col + (d_depth[j] * d_depth[j] + 4.0)
                    light = 0.3 + jnp.abs(facing) * lax.rsqrt(norm)
                    total[j] = total[j] + ext
                    after = jnp.exp2(total[j] * K_EXT)
                    part = (trans[j] - after) * light
                    trans[j] = after
                    weight[j] = weight[j] + part
                    for c in range(3):
                        tone = jnp.tanh(warm[j] * tint_s[z, c] + tint_s[z, 3 + c])
                        tinted[c][j] = tinted[c][j] + part * tone
            spot = pl.ds(pl.multiple_of(step * rows, rows) + at, GROUP)
            for j in range(parts):
                for c in range(4):
                    value = 0.5 * (weight[j] + tinted[c][j]) if c < 3 else total[j]
                    if partial is None:
                        acc_s[c, block * parts + j, spot, :] = value
                    else:
                        v = pl.ds(pl.multiple_of(base + 128 * j, 128), 128)
                        partial[c, at : at + GROUP, v] = value
            return 0

        lax.fori_loop(0, cols // COLS_STEP, columns, 0, unroll=UNROLL)

    if partial is not None:
        return
    wide, _, count, _ = send.shape

    @pl.when(step == pl.num_programs(0) - 1)
    def _():
        def destination(to, _):
            for channel in range(4):
                for column in range(cols // 128):
                    value = acc_s[channel, column, pl.ds(to, count, wide), :]
                    w = pl.ds(128 * column, 128)
                    send[to, channel, :, w] = encode(value, tops(channel))
            return 0

        lax.fori_loop(0, wide, destination, 0)


def finish_kernel(codes, *rest):
    image = rest[-1]
    wide, _, count, cols = codes.shape

    def columns(column, _):
        w = pl.ds(pl.multiple_of(128 * column, 128), 128)
        total = jnp.zeros((count, 128), jnp.float32)
        color = [total] * 3
        trans = jnp.ones_like(total)
        for source in range(wide):
            color = [
                color[c] + trans * decode(codes[source, c, :, w], TOP_COLOR) for c in range(3)
            ]
            total = total + decode(codes[source, 3, :, w], TOP_EXT)
            trans = jnp.exp2(total * K_EXT)
        for c in range(3):
            image[:, c, w] = color[c]
        image[:, 3, w] = 1.0 - trans
        return 0

    lax.fori_loop(0, cols // 128, columns, 0)


def pieces(value, count):
    parts = []
    for _ in range(count):
        part = lax.reduce_precision(value, 8, 7)
        parts.append(part)
        value = value - part
    return parts


def bump_table(means, widths, heights):
    square = widths * widths * LOG2E
    none = jnp.zeros_like(means)
    a = pieces(-square, 3)
    b = pieces(2.0 * square * means, 3)
    c = pieces(jnp.log2(heights) - square * means * means, 3)
    table = jnp.stack([*a, *a[:2], *b, *c, none, none], axis=2)
    return jnp.repeat(table, GROUP, axis=2)


def row_differences():
    r = jnp.arange(GROUP)[:, None]
    lane = jnp.arange(WIDTH)[None, :]
    block, line = lane // GROUP, lane % GROUP
    plus = ((block == 5) & (line == r + 1)) | ((block == 12) & (line == 0) & (r == GROUP - 1))
    minus = ((block == 5) & (line == r - 1)) | ((block == 11) & (line == GROUP - 1) & (r == 0))
    return (plus.astype(jnp.float32) - minus.astype(jnp.float32)).astype(jnp.bfloat16)


def shade(mode, at, size, wide, mass, edges, heat, tables, halo=(), inner=()):
    depth, rows, cols = mass.shape
    lanes, picks, table, tint, row_diff = tables
    block = ROW_BLOCK
    steps = size // block
    per = block // GROUP
    start = at // block
    in_specs = [
        pl.BlockSpec((depth, block, cols), lambda i: (0, start + i, 0)),
        pl.BlockSpec(
            (depth, GROUP, cols), lambda i: (0, jnp.maximum((start + i) * per - 1, 0), 0)
        ),
        pl.BlockSpec(
            (depth, GROUP, cols),
            lambda i: (0, jnp.minimum((start + i + 1) * per, rows // GROUP - 1), 0),
        ),
        pl.BlockSpec((depth, 1, cols), lambda i: (0, 0, 0)),
        pl.BlockSpec((depth, 1, cols), lambda i: (0, 0, 0)),
        pl.BlockSpec((depth, block, cols), lambda i: (0, start + i, 0)),
        pl.BlockSpec((depth, per, 1, WIDTH), lambda i: (0, start + i, 0, 0)),
        pl.BlockSpec((depth, size), lambda i: (0, at // size)),
        pl.BlockSpec(table.shape, lambda i: (0, 0, 0)),
        pl.BlockSpec(tint.shape, lambda i: (0, 0)),
        pl.BlockSpec((GROUP, WIDTH), lambda i: (0, 0)),
    ]
    for _ in halo:
        in_specs.append(pl.BlockSpec((1, block, cols), lambda i: (0, start + i, 0)))
    for _ in inner:
        in_specs.append(pl.BlockSpec((4, block, cols), lambda i: (0, i, 0)))
    scratch = [
        pltpu.VMEM((depth, GROUP * (table.shape[1] + 1), WIDTH), jnp.bfloat16),
        pltpu.VMEM((depth, 6, GROUP, 128), jnp.float32),
        pltpu.VMEM((size, depth), jnp.int32),
        pltpu.VMEM((2, depth, GROUP, cols), jnp.bfloat16),
    ]
    if mode == "inner":
        out_specs = pl.BlockSpec((4, block, cols), lambda i: (0, i, 0))
        out_shape = jax.ShapeDtypeStruct((4, size, cols), jnp.float32)
    else:
        shape = (wide, 4, size // wide, cols)
        out_specs = pl.BlockSpec(shape, lambda i: (0, 0, 0, 0))
        out_shape = jax.ShapeDtypeStruct(shape, jnp.int16)
        scratch.append(pltpu.VMEM((4, cols // 128, size, 128), jnp.float32))
    layers = {"full": depth, "inner": depth - 2, "outer": 2}[mode]
    cells = size * cols * layers
    return pl.pallas_call(
        functools.partial(shade_kernel, mode, at == 0, at + size == rows),
        grid=(steps,),
        in_specs=in_specs,
        out_specs=out_specs,
        out_shape=out_shape,
        scratch_shapes=scratch,
        name=f"shade_{mode}",
        cost_estimate=pl.CostEstimate(
            flops=cells * 90, bytes_accessed=cells * 6, transcendentals=cells * 13
        ),
    )(mass, mass, mass, *edges, heat, lanes, picks, table, tint, row_diff, *halo, *inner)


def finish(at, rows, codes, image):
    wide, _, count, cols = codes.shape
    whole = pl.BlockSpec((wide, 4, count, cols), lambda i: (0, 0, 0, 0))
    args, specs, alias = [codes], [whole], {}
    if image is not None:
        args.append(image)
        specs.append(pl.BlockSpec(memory_space=pl.ANY))
        alias = {1: 0}
    return pl.pallas_call(
        finish_kernel,
        grid=(1,),
        in_specs=specs,
        out_specs=pl.BlockSpec((count, 4, cols), lambda i: (at // wide // count, 0, 0)),
        out_shape=jax.ShapeDtypeStruct((rows // wide, 4, cols), jnp.float32),
        input_output_aliases=alias,
        name="finish",
        cost_estimate=pl.CostEstimate(
            flops=wide * count * cols * 40,
            bytes_accessed=wide * count * cols * 8,
            transcendentals=wide * count * cols * 5,
        ),
    )(*args)


def per_device(mass, heat, picks, means, widths, heights, tint):
    depth, rows, cols = mass.shape
    wide = lax.axis_size("wide")
    narrow = lax.axis_size("narrow")
    half = rows // PARTS

    def swap(value, axis, step):
        count = lax.axis_size(axis)
        pairs = [(i, i + step) for i in range(count) if 0 <= i + step < count]
        return lax.ppermute(value, axis, pairs)

    edges = (swap(mass[:, rows - 1 :, :], "narrow", 1), swap(mass[:, :1, :], "narrow", -1))
    halo = (swap(mass[depth - 1 :], "wide", 1), swap(mass[:1], "wide", -1))

    lanes = jnp.tile(picks.reshape(depth, rows // GROUP, 1, GROUP), (1, 1, 1, BLOCKS))
    table = bump_table(means, widths, heights)
    tint = jnp.pad(0.5 * tint, ((0, 0), (0, 128 - tint.shape[1])))
    tables = (lanes, picks, table, tint, row_differences())

    inner = shade("inner", 0, half, wide, mass, edges, heat, tables)
    sends = [shade("outer", 0, half, wide, mass, edges, heat, tables, halo, (inner,))]
    for part in range(1, PARTS):
        lanes, sends[-1] = lax.optimization_barrier((tables[0], sends[-1]))
        tables = (lanes, *tables[1:])
        sends.append(shade("full", part * half, half, wide, mass, edges, heat, tables, halo))
    image = None
    for part, send in enumerate(sends):
        received = lax.all_to_all(send, "wide", 0, 0, tiled=True)
        image = finish(part * half, rows, received, image)
    return image.reshape(1, rows // wide, 1, 4, cols)


def solution(mesh):
    return jax.shard_map(
        per_device,
        mesh=mesh,
        in_specs=(
            P("wide", "narrow", None),
            P("wide", "narrow", None),
            P("wide", "narrow"),
            P(),
            P(),
            P(),
            P(),
        ),
        out_specs=P("narrow", None, "wide", None, None),
        check_vma=False,
    )
```

```python
import functools
import math

import jax
import jax.numpy as jnp
from jax import lax
from jax.experimental import pallas as pl
from jax.experimental.pallas import tpu as pltpu
from jax.sharding import PartitionSpec as P

STEP = 0.003
LOG2E = math.log2(math.e)
SHADE = 0.7
L_DEPTH, L_ROWS, L_COLS = 0.64 * SHADE, 0.6 * SHADE, 0.48 * SHADE
K_EXT = -STEP * LOG2E

OCTAVES = 22.0
SCALE = 65534.0 / OCTAVES
TOP = 0.0

PARTS = 2
ROW_BLOCK = 32
COLS_STEP = 256
GROUP = 16
BLOCKS = 16
WIDTH = BLOCKS * GROUP
UNROLL = 2
PERMUTES = 8
VMEM_BYTES = 67000000


def encode(value):
    code = jnp.log2(value) * SCALE + ((OCTAVES - TOP) * SCALE + 1.5)
    return (jnp.maximum(code, 0.0).astype(jnp.int32) - 32768).astype(jnp.int16)


def decode(code):
    code = code.astype(jnp.int32).astype(jnp.float32)
    value = jnp.exp2(code * (1.0 / SCALE) + (TOP - OCTAVES + 32767.0 / SCALE))
    return jnp.where(code > -32768.0, value, 0.0)


def pieces(value, count):
    parts = []
    for _ in range(count):
        part = value.astype(jnp.bfloat16).astype(jnp.float32)
        parts.append(part)
        value = value - part
    return parts


def fill_tables(means, widths, heights, tint, table_s):
    tables = means.shape[0]
    bumps = means.shape[1]
    square = pieces((widths[...] * widths[...] * LOG2E).T, 2)
    mean = means[...].T
    both = square[0] + square[1]
    a = [-part for part in square]
    b = pieces(2.0 * both * mean, 3)
    c = pieces(jnp.log2(heights[...]).T + math.log2(-K_EXT) - both * mean * mean, 3)
    shade_columns = [*a, *a, *b, *c]
    color = 0.5 * tint[...].T
    scale, offset = pieces(color[:3], 3), pieces(color[3:], 3)
    tint_columns = [None] * 7 + [*offset, *scale]
    block = lax.broadcasted_iota(jnp.int32, (bumps, WIDTH), 1) // GROUP

    def row(columns, t, count):
        value = jnp.zeros((count, WIDTH), jnp.float32)
        for k, column in enumerate(columns):
            if column is not None:
                wide = jnp.broadcast_to(column[:, t : t + 1], (count, WIDTH))
                value = jnp.where(block[:count] == k, wide, value)
        return value

    for t in range(tables):
        table_s[t, :bumps] = row(shade_columns, t, bumps)
        table_s[t, bumps : bumps + 3] = row(tint_columns, t, 3)


def differences():
    shape = (GROUP, WIDTH)
    r = lax.broadcasted_iota(jnp.int32, shape, 0)
    lane = lax.broadcasted_iota(jnp.int32, shape, 1)
    block, line = lane // GROUP, lane % GROUP
    mid, around, left, right = 4, 13, 14, 15
    plus = ((block == mid) & (line == r + 1)) | (
        (block == around) & (line == 0) & (r == GROUP - 1)
    )
    minus = ((block == mid) & (line == r - 1)) | (
        (block == around) & (line == GROUP - 1) & (r == 0)
    )
    rows = jnp.where(plus, 1.0, jnp.where(minus, -1.0, 0.0))
    same = line == r
    cols = jnp.where(
        (block == right) & same, 1.0, jnp.where((block == left) & same, -1.0, 0.0)
    )
    return rows.astype(jnp.bfloat16), cols.astype(jnp.bfloat16)


def shade_kernel(mode, first, last, start, *refs):
    mass, above, below, outer_up, outer_down, heat, picks, means, widths, heights, tint = refs[:11]
    refs = refs[11:]
    low = high = inner = partial = None
    if mode != "inner":
        low, high, *refs = refs
    if mode == "outer":
        inner, *refs = refs
    if mode == "inner":
        partial, a_s, table_s, lanes_s = refs
    else:
        *sends, a_s, table_s, lanes_s, acc_s = refs
    step = pl.program_id(0)
    depth, rows, cols = mass.shape
    tables, bumps = means.shape
    outs = bumps + 3
    groups = rows // GROUP
    parts = COLS_STEP // 128
    layers = {"full": range(depth), "inner": range(1, depth - 1), "outer": (0, depth - 1)}[mode]

    @pl.when(step == 0)
    def _():
        fill_tables(means, widths, heights, tint, table_s)
        by_row, by_col = differences()
        for z in layers:
            a_s[z, GROUP * outs : GROUP * (outs + 1)] = by_row
            a_s[z, GROUP * (outs + 1) :] = by_col
        spot = lax.broadcasted_iota(jnp.int32, (depth, 128), 1)
        for q in range(lanes_s.shape[0]):
            line = start + q * GROUP
            value = picks[:, line // 128 * 128 : line // 128 * 128 + 128]
            if line % 128:
                value = pltpu.roll(value, 128 - line % 128, 1)
            value = jnp.where(spot < GROUP, value, 0)
            for shift in (16, 32, 64):
                value = value + pltpu.roll(value, shift, 1)
            lanes_s[q] = value

    diagonal = lax.broadcasted_iota(jnp.int32, (GROUP, WIDTH), 1) % GROUP == (
        lax.broadcasted_iota(jnp.int32, (GROUP, WIDTH), 0)
    )
    lane = lax.broadcasted_iota(jnp.int16, (GROUP, 128), 1)
    ones = jnp.ones((GROUP, COLS_STEP), jnp.bfloat16)

    for group in range(groups):
        at = GROUP * group

        for z in layers:
            chosen = jnp.broadcast_to(lanes_s[step * groups + group, z : z + 1, :], (16, 128))
            chosen = jnp.concatenate([chosen, chosen], axis=1)
            line = table_s[0]
            for t in range(1, tables):
                line = jnp.where(chosen == t, table_s[t], line)
            for k in range(outs):
                wide = jnp.broadcast_to(line[k : k + 1], (GROUP, WIDTH))
                a_s[z, GROUP * k : GROUP * (k + 1)] = jnp.where(diagonal, wide, 0.0).astype(
                    jnp.bfloat16
                )

        def columns(block, _, at=at, group=group):
            base = pl.multiple_of(COLS_STEP * block, COLS_STEP)
            w = pl.ds(base, COLS_STEP)
            before = pl.ds(pl.multiple_of(jnp.maximum(base - 128, 0), 128), 128)
            beyond = pl.ds(
                pl.multiple_of(jnp.minimum(base + COLS_STEP, cols - 128), 128), 128
            )
            planes = {}

            def plane16(z):
                if z not in planes:
                    if z < 0:
                        planes[z] = low[0, at : at + GROUP, w]
                    elif z == depth:
                        planes[z] = high[0, at : at + GROUP, w]
                    else:
                        planes[z] = mass[z, at : at + GROUP, w]
                return planes[z]

            wides = {}

            def plane(z):
                if z not in wides:
                    wides[z] = plane16(z).astype(jnp.float32)
                return wides[z]

            def split(value):
                return [value[:, 128 * j : 128 * (j + 1)] for j in range(parts)]

            def tile(z, part, outside):
                value = mass[z, at : at + GROUP, part]
                return jnp.where(outside, jnp.zeros_like(value), value)

            def around(z):
                half = GROUP // 2
                up = above[z, :, w] if group == 0 else mass[z, at - half : at, w]
                if group == 0 and first:
                    up = jnp.where(
                        step == 0, jnp.broadcast_to(outer_up[z, :, w], up.shape), up
                    )
                if group < groups - 1:
                    down = mass[z, at + GROUP : at + GROUP + half, w]
                else:
                    down = below[z, :, w]
                    if last:
                        down = jnp.where(
                            step == pl.num_programs(0) - 1,
                            jnp.broadcast_to(outer_down[z, :, w], down.shape),
                            down,
                        )
                return jnp.concatenate([down, up], axis=0)

            one = jnp.ones((GROUP, 128), jnp.float32)
            zero = jnp.zeros((GROUP, 128), jnp.float32)
            trans = [one] * parts
            total = [zero] * parts
            weight = [zero] * parts
            tinted = [[zero] * parts for _ in range(3)]
            for z in layers:
                if mode == "outer" and z:
                    for j in range(parts):
                        v = pl.ds(pl.multiple_of(base + 128 * j, 128), 128)
                        for c in range(3):
                            within = inner[c, at : at + GROUP, v]
                            tinted[c][j] = tinted[c][j] + (2.0 * trans[j]) * within
                        total[j] = total[j] + inner[3, at : at + GROUP, v]
                        trans[j] = jnp.exp2(total[j])
                current16 = plane16(z)
                square = plane(z) * plane(z)
                high16 = square.astype(jnp.bfloat16)
                low16 = (square - high16.astype(jnp.float32)).astype(jnp.bfloat16)
                heat16 = heat[z, at : at + GROUP, w]
                mids = [
                    tile(z, before, block == 0),
                    *split(current16),
                    tile(z, beyond, block == cols // COLS_STEP - 1),
                ]
                to_right = [pltpu.roll(v, 1, 1) for v in mids[:-1]]
                to_left = [pltpu.roll(v, 127, 1) for v in mids[1:]]
                left16 = jnp.concatenate(
                    [jnp.where(lane == 0, to_right[j], to_right[j + 1]) for j in range(parts)], 1
                )
                right16 = jnp.concatenate(
                    [jnp.where(lane == 127, to_left[j + 1], to_left[j]) for j in range(parts)], 1
                )
                stacked = jnp.concatenate(
                    [high16] * 2 + [low16] * 2 + [current16] * 3 + [ones] * 3 + [heat16] * 3
                    + [around(z), left16, right16],
                    axis=0,
                )
                product = jnp.dot(a_s[z], stacked, preferred_element_type=jnp.float32)
                d_depth = split(plane(z + 1) - plane(z - 1))
                for j in range(parts):
                    def out(k):
                        return product[GROUP * k : GROUP * (k + 1), 128 * j : 128 * (j + 1)]

                    ext = jnp.exp2(out(0))
                    for g in range(1, bumps):
                        ext = ext + jnp.exp2(out(g))
                    d_row, d_col = out(outs), out(outs + 1)
                    facing = d_row * L_ROWS + d_col * L_COLS + d_depth[j] * L_DEPTH
                    norm = d_row * d_row + d_col * d_col + (d_depth[j] * d_depth[j] + 4.0)
                    light = 0.3 + jnp.abs(facing) * lax.rsqrt(norm)
                    total[j] = total[j] - ext
                    after = jnp.exp2(total[j])
                    part = (trans[j] - after) * light
                    trans[j] = after
                    weight[j] = weight[j] + part
                    for c in range(3):
                        tinted[c][j] = tinted[c][j] + part * jnp.tanh(out(bumps + c))
            spot = pl.ds(pl.multiple_of(step * rows, rows) + at, GROUP)
            for j in range(parts):
                for c in range(4):
                    value = 0.5 * (weight[j] + tinted[c][j]) if c < 3 else total[j]
                    if partial is None:
                        acc_s[c, block * parts + j, spot, :] = value if c < 3 else -value
                    else:
                        v = pl.ds(pl.multiple_of(base + 128 * j, 128), 128)
                        partial[c, at : at + GROUP, v] = value
            return 0

        unroll = 2 * UNROLL if mode == "outer" else UNROLL
        lax.fori_loop(0, cols // COLS_STEP, columns, 0, unroll=unroll)

    if partial is not None:
        return
    @pl.when(step == pl.num_programs(0) - 1)
    def _():
        wide = len(sends) if len(sends) > 1 else sends[0].shape[0]
        count = sends[0].shape[-2]

        def store(out, to):
            def channels(channel, _):
                for column in range(cols // 128):
                    value = acc_s[channel, column, pl.ds(to, count, wide), :]
                    out[channel, :, 128 * column : 128 * (column + 1)] = encode(value)
                return 0

            lax.fori_loop(0, 4, channels, 0)

        if len(sends) > 1:
            me = lax.axis_index("wide")
            for k, out in enumerate(sends):
                store(out, jnp.bitwise_xor(me, k))
        else:
            lax.fori_loop(0, wide, lambda to, _: store(sends[0].at[to], to) or 0, 0)


def finish_kernel(parts, *refs):
    image, codes, sems = refs[-3:]
    if parts > 1:
        me = lax.axis_index("wide")
        copies = [
            pltpu.make_async_copy(refs[k], codes.at[jnp.bitwise_xor(me, k)], sems.at[k])
            for k in range(parts)
        ]
    else:
        copies = [pltpu.make_async_copy(refs[0], codes, sems.at[0])]
    for copy in copies:
        copy.start()
    for copy in copies:
        copy.wait()
    wide, _, count, cols = codes.shape

    def columns(column, _):
        w = pl.ds(pl.multiple_of(128 * column, 128), 128)
        total = jnp.zeros((count, 128), jnp.float32)
        color = [total] * 3
        trans = jnp.ones_like(total)
        for source in range(wide):
            color = [color[c] + trans * decode(codes[source, c, :, w]) for c in range(3)]
            total = total - decode(codes[source, 3, :, w])
            trans = jnp.exp2(total)
        for c in range(3):
            image[:, c, w] = color[c]
        image[:, 3, w] = 1.0 - trans
        return 0

    lax.fori_loop(0, cols // 128, columns, 0, unroll=2)


def shade(mode, at, size, wide, mass, edges, heat, tables, halo=(), inner=()):
    depth, rows, cols = mass.shape
    bumps = tables[1].shape[1]
    block = ROW_BLOCK
    steps = size // block
    per8 = block // 8
    start = at // block
    in_specs = [
        pl.BlockSpec((depth, block, cols), lambda i: (0, start + i, 0)),
        pl.BlockSpec((depth, 8, cols), lambda i: (0, jnp.maximum((start + i) * per8 - 1, 0), 0)),
        pl.BlockSpec(
            (depth, 8, cols),
            lambda i: (0, jnp.minimum((start + i + 1) * per8, rows // 8 - 1), 0),
        ),
        pl.BlockSpec((depth, 1, cols), lambda i: (0, 0, 0)),
        pl.BlockSpec((depth, 1, cols), lambda i: (0, 0, 0)),
        pl.BlockSpec((depth, block, cols), lambda i: (0, start + i, 0)),
        *[pl.BlockSpec(value.shape, lambda i: (0, 0)) for value in tables],
    ]
    for _ in halo:
        in_specs.append(pl.BlockSpec((1, block, cols), lambda i: (0, start + i, 0)))
    for _ in inner:
        in_specs.append(pl.BlockSpec((4, block, cols), lambda i: (0, i, 0)))
    scratch = [
        pltpu.VMEM((depth, GROUP * (bumps + 5), WIDTH), jnp.bfloat16),
        pltpu.VMEM((tables[1].shape[0], 16, WIDTH), jnp.float32),
        pltpu.VMEM((size // GROUP, depth, 128), jnp.int32),
    ]
    if mode == "inner":
        out_specs = pl.BlockSpec((4, block, cols), lambda i: (0, i, 0))
        out_shape = jax.ShapeDtypeStruct((4, size, cols), jnp.float32)
    else:
        shape = (4, size // wide, cols)
        if wide > PERMUTES:
            out_specs = [pl.BlockSpec((wide, *shape), lambda i: (0, 0, 0, 0))]
            out_shape = [jax.ShapeDtypeStruct((wide, *shape), jnp.int16)]
        else:
            out_specs = [pl.BlockSpec(shape, lambda i: (0, 0, 0))] * wide
            out_shape = [jax.ShapeDtypeStruct(shape, jnp.int16)] * wide
        scratch.append(pltpu.VMEM((4, cols // 128, size, 128), jnp.float32))
    layers = {"full": depth, "inner": depth - 2, "outer": 2}[mode]
    cells = size * cols * layers
    return pl.pallas_call(
        functools.partial(shade_kernel, mode, at == 0, at + size == rows, at),
        grid=(steps,),
        in_specs=in_specs,
        out_specs=out_specs,
        out_shape=out_shape,
        scratch_shapes=scratch,
        name=f"shade_{mode}",
        compiler_params=pltpu.CompilerParams(vmem_limit_bytes=VMEM_BYTES),
        cost_estimate=pl.CostEstimate(
            flops=cells * 90, bytes_accessed=cells * 6, transcendentals=cells * 13
        ),
    )(mass, mass, mass, *edges, heat, *tables, *halo, *inner)


def finish(at, size, rows, wide, codes, image):
    count, cols = codes[0].shape[-2:]
    args, alias = [*codes], {}
    if image is not None:
        alias = {len(args): 0}
        args.append(image)
    cells = size * cols
    return pl.pallas_call(
        functools.partial(finish_kernel, len(codes)),
        grid=(1,),
        in_specs=[pl.BlockSpec(memory_space=pl.ANY)] * len(args),
        out_specs=pl.BlockSpec((count, 4, cols), lambda i: (at // size, 0, 0)),
        out_shape=jax.ShapeDtypeStruct((rows // wide, 4, cols), jnp.float32),
        scratch_shapes=[
            pltpu.VMEM((wide, 4, count, cols), jnp.int16),
            pltpu.SemaphoreType.DMA((len(codes),)),
        ],
        input_output_aliases=alias,
        name="finish",
        compiler_params=pltpu.CompilerParams(vmem_limit_bytes=VMEM_BYTES),
        cost_estimate=pl.CostEstimate(
            flops=cells * 40, bytes_accessed=cells * 8, transcendentals=cells * 5
        ),
    )(*args)


def exchange(sends):
    if len(sends) == 1:
        return [lax.all_to_all(sends[0], "wide", 0, 0, tiled=True)]
    wide = len(sends)
    received = [sends[0]]
    for k in range(1, wide):
        received.append(lax.ppermute(sends[k], "wide", [(i, i ^ k) for i in range(wide)]))
    return received


def per_device(mass, heat, picks, means, widths, heights, tint):
    depth, rows, cols = mass.shape
    wide = lax.axis_size("wide")
    narrow = lax.axis_size("narrow")
    half = rows // PARTS

    def swap(value, axis, step):
        count = lax.axis_size(axis)
        pairs = [(i, i + step) for i in range(count) if 0 <= i + step < count]
        return lax.ppermute(value, axis, pairs)

    halo = (swap(mass[depth - 1 :], "wide", 1), swap(mass[:1], "wide", -1))
    edges = (swap(mass[:, rows - 1 :, :], "narrow", 1), swap(mass[:, :1, :], "narrow", -1))

    tables = (picks, means, widths, heights, tint)
    inner = shade("inner", 0, half, wide, mass, edges, heat, tables)
    sends = [shade("outer", 0, half, wide, mass, edges, heat, tables, halo, (inner,))]
    for part in range(1, PARTS):
        means, *sends[-1] = lax.optimization_barrier((means, *sends[-1]))
        tables = (picks, means, widths, heights, tint)
        sends.append(shade("full", part * half, half, wide, mass, edges, heat, tables, halo))
    image = None
    for part, send in enumerate(sends):
        image = finish(part * half, half, rows, wide, exchange(send), image)
    return image.reshape(1, rows // wide, 1, 4, cols)


def solution(mesh):
    return jax.shard_map(
        per_device,
        mesh=mesh,
        in_specs=(
            P("wide", "narrow", None),
            P("wide", "narrow", None),
            P("wide", "narrow"),
            P(),
            P(),
            P(),
            P(),
        ),
        out_specs=P("narrow", None, "wide", None, None),
        check_vma=False,
    )
```

```python
import functools
import math

import jax
import jax.numpy as jnp
from jax import lax
from jax.experimental import pallas as pl
from jax.experimental.pallas import tpu as pltpu
from jax.sharding import PartitionSpec as P


STEP = 0.003
LOG2E = math.log2(math.e)
SHADE = 0.7
L_DEPTH, L_ROWS, L_COLS = 0.64 * SHADE, 0.6 * SHADE, 0.48 * SHADE
K_EXT = -STEP * LOG2E

OCTAVES = 22.0
SCALE = 65534.0 / OCTAVES
TOP = 0.0

ROW_BLOCK = 32
COLS_STEP = 256
GROUP = 16
BLOCKS = 13
WIDTH = BLOCKS * GROUP
UNROLL = 4
PERMUTES = 8
VMEM_BYTES = 67000000


def encode(value):
    code = jnp.log2(value) * SCALE + ((OCTAVES - TOP) * SCALE + 1.5)
    return (jnp.maximum(code, 0.0).astype(jnp.int32) - 32768).astype(jnp.int16)


def decode(code):
    code = code.astype(jnp.int32).astype(jnp.float32)
    value = jnp.exp2(code * (1.0 / SCALE) + (TOP - OCTAVES + 32767.0 / SCALE))
    return jnp.where(code > -32768.0, value, 0.0)


def pieces(value, count):
    parts = []
    for _ in range(count):
        part = value.astype(jnp.bfloat16).astype(jnp.float32)
        parts.append(part)
        value = value - part
    return parts


def fill_tables(means, widths, heights, tint, table_s):
    tables = means.shape[0]
    bumps = means.shape[1]
    square = pieces((widths[...] * widths[...] * LOG2E).T, 2)
    mean = means[...].T
    both = square[0] + square[1]
    a = [-part for part in square]
    b = pieces(2.0 * both * mean, 3)
    c = pieces(jnp.log2(heights[...]).T + math.log2(-K_EXT) - both * mean * mean, 3)
    shade_columns = [*a, *a, *b, *c]
    color = 0.5 * tint[...].T
    scale, offset = pieces(color[:3], 2), pieces(color[3:], 3)
    tint_columns = [None] * 7 + [*offset, *scale]
    block = lax.broadcasted_iota(jnp.int32, (bumps, WIDTH), 1) // GROUP

    def row(columns, t, count):
        value = jnp.zeros((count, WIDTH), jnp.float32)
        for k, column in enumerate(columns):
            if column is not None:
                wide = jnp.broadcast_to(column[:, t : t + 1], (count, WIDTH))
                value = jnp.where(block[:count] == k, wide, value)
        return value

    for t in range(tables):
        table_s[t, :bumps] = row(shade_columns, t, bumps)
        table_s[t, bumps : bumps + 3] = row(tint_columns, t, 3)


def row_differences():
    shape = (GROUP, WIDTH)
    r = lax.broadcasted_iota(jnp.int32, shape, 0)
    lane = lax.broadcasted_iota(jnp.int32, shape, 1)
    block, line = lane // GROUP, lane % GROUP
    mid, around = 4, 12
    plus = ((block == mid) & (line == r + 1)) | (
        (block == around) & (line == 0) & (r == GROUP - 1)
    )
    minus = ((block == mid) & (line == r - 1)) | (
        (block == around) & (line == GROUP - 1) & (r == 0)
    )
    rows = jnp.where(plus, 1.0, jnp.where(minus, -1.0, 0.0))
    return rows.astype(jnp.bfloat16)


def shade_kernel(mode, ends, lines, *refs):
    mass, above, below, heat, picks, means, widths, heights, tint, *refs = refs
    low = high = inner = partial = None
    if ends:
        outer_up, outer_down, *refs = refs
    if mode != "inner":
        low, high, *refs = refs
    if mode == "outer":
        inner, *refs = refs
    if mode == "inner":
        partial, a_s, table_s, lanes_s = refs
    else:
        *sends, a_s, table_s, lanes_s, acc_s = refs
    step = pl.program_id(0)
    depth, rows, cols = mass.shape
    tables, bumps = means.shape
    outs = bumps + 3
    groups = rows // GROUP
    parts = COLS_STEP // 128
    layers = {"full": range(depth), "inner": range(1, depth - 1), "outer": (0, depth - 1)}[mode]

    @pl.when(step == 0)
    def _():
        fill_tables(means, widths, heights, tint, table_s)
        by_row = row_differences()
        for z in layers:
            for group in range(groups):
                a_s[group, z, GROUP * outs :] = by_row
        spot = lax.broadcasted_iota(jnp.int32, (depth, 128), 1)
        for q, line in enumerate(lines):
            value = picks[:, line // 128 * 128 : line // 128 * 128 + 128]
            if line % 128:
                value = pltpu.roll(value, 128 - line % 128, 1)
            value = jnp.where(spot < GROUP, value, 0)
            for shift in (16, 32, 64):
                value = value + pltpu.roll(value, shift, 1)
            lanes_s[q] = value

    diagonal = lax.broadcasted_iota(jnp.int32, (GROUP, WIDTH), 1) % GROUP == (
        lax.broadcasted_iota(jnp.int32, (GROUP, WIDTH), 0)
    )
    lane = lax.broadcasted_iota(jnp.int16, (GROUP, 128), 1)
    ones = jnp.ones((GROUP, COLS_STEP), jnp.bfloat16)

    for group in range(groups):
        at = GROUP * group

        for z in layers:
            chosen = jnp.broadcast_to(lanes_s[step * groups + group, z : z + 1, :], (16, 128))
            chosen = jnp.concatenate([chosen, chosen[:, : WIDTH - 128]], axis=1)
            line = table_s[0]
            for t in range(1, tables):
                line = jnp.where(chosen == t, table_s[t], line)
            for k in range(outs):
                wide = jnp.broadcast_to(line[k : k + 1], (GROUP, WIDTH))
                a_s[group, z, GROUP * k : GROUP * (k + 1)] = jnp.where(diagonal, wide, 0.0).astype(
                    jnp.bfloat16
                )

        def columns(block, _, at=at, group=group):
            base = pl.multiple_of(COLS_STEP * block, COLS_STEP)
            w = pl.ds(base, COLS_STEP)
            before = pl.ds(pl.multiple_of(jnp.maximum(base - 128, 0), 128), 128)
            beyond = pl.ds(
                pl.multiple_of(jnp.minimum(base + COLS_STEP, cols - 128), 128), 128
            )
            planes = {}

            def plane16(z):
                if z not in planes:
                    if z < 0:
                        planes[z] = low[0, at : at + GROUP, w]
                    elif z == depth:
                        planes[z] = high[0, at : at + GROUP, w]
                    else:
                        planes[z] = mass[z, at : at + GROUP, w]
                return planes[z]

            wides = {}

            def plane(z):
                if z not in wides:
                    wides[z] = plane16(z).astype(jnp.float32)
                return wides[z]

            def split(value):
                return [value[:, 128 * j : 128 * (j + 1)] for j in range(parts)]

            def tile(z, part, outside):
                value = mass[z, at : at + GROUP, part]
                return jnp.where(outside, jnp.zeros_like(value), value)

            def around(z):
                half = GROUP // 2
                up = above[z, :, w] if group == 0 else mass[z, at - half : at, w]
                if group == 0 and ends:
                    up = jnp.where(step == 0, outer_up[z, :, w], up)
                if group < groups - 1:
                    down = mass[z, at + GROUP : at + GROUP + half, w]
                else:
                    down = below[z, :, w]
                    if ends:
                        last_step = step == pl.num_programs(0) - 1
                        down = jnp.where(last_step, outer_down[z, :, w], down)
                return jnp.concatenate([down, up], axis=0)

            one = jnp.ones((GROUP, 128), jnp.float32)
            zero = jnp.zeros((GROUP, 128), jnp.float32)
            trans = [one] * parts
            total = [zero] * parts
            weight = [zero] * parts
            tinted = [[zero] * parts for _ in range(3)]
            for z in layers:
                if mode == "outer" and z:
                    for j in range(parts):
                        v = pl.ds(pl.multiple_of(base + 128 * j, 128), 128)
                        for c in range(3):
                            within = inner[c, at : at + GROUP, v]
                            tinted[c][j] = tinted[c][j] + (2.0 * trans[j]) * within
                        total[j] = total[j] + inner[3, at : at + GROUP, v]
                        trans[j] = jnp.exp2(total[j])
                current16 = plane16(z)
                square = plane(z) * plane(z)
                high16 = square.astype(jnp.bfloat16)
                low16 = (square - high16.astype(jnp.float32)).astype(jnp.bfloat16)
                heat16 = heat[z, at : at + GROUP, w]
                mids = [
                    tile(z, before, block == 0),
                    *split(current16),
                    tile(z, beyond, block == cols // COLS_STEP - 1),
                ]
                to_right = [pltpu.roll(v, 1, 1) for v in mids[:-1]]
                to_left = [pltpu.roll(v, 127, 1) for v in mids[1:]]
                lefts = [jnp.where(lane == 0, to_right[j], to_right[j + 1]) for j in range(parts)]
                rights = [
                    jnp.where(lane == 127, to_left[j + 1], to_left[j]) for j in range(parts)
                ]
                stacked = jnp.concatenate(
                    [high16] * 2 + [low16] * 2 + [current16] * 3 + [ones] * 3 + [heat16] * 2
                    + [around(z)],
                    axis=0,
                )
                product = jnp.dot(a_s[group, z], stacked, preferred_element_type=jnp.float32)
                d_depth = split(plane(z + 1) - plane(z - 1))
                for j in range(parts):
                    def out(k):
                        return product[GROUP * k : GROUP * (k + 1), 128 * j : 128 * (j + 1)]

                    ext = jnp.exp2(out(0))
                    for g in range(1, bumps):
                        ext = ext + jnp.exp2(out(g))
                    d_row = out(outs)
                    d_col = rights[j].astype(jnp.float32) - lefts[j].astype(jnp.float32)
                    facing = d_row * L_ROWS + d_col * L_COLS + d_depth[j] * L_DEPTH
                    norm = d_row * d_row + d_col * d_col + (d_depth[j] * d_depth[j] + 4.0)
                    light = 0.3 + jnp.abs(facing) * lax.rsqrt(norm)
                    total[j] = total[j] - ext
                    after = jnp.exp2(total[j])
                    part = (trans[j] - after) * light
                    trans[j] = after
                    weight[j] = weight[j] + part
                    for c in range(3):
                        tinted[c][j] = tinted[c][j] + part * jnp.tanh(out(bumps + c))
            spot = pl.ds(pl.multiple_of(step * rows, rows) + at, GROUP)
            for j in range(parts):
                for c in range(4):
                    value = 0.5 * (weight[j] + tinted[c][j]) if c < 3 else total[j]
                    if partial is None:
                        acc_s[c, block * parts + j, spot, :] = value if c < 3 else -value
                    else:
                        v = pl.ds(pl.multiple_of(base + 128 * j, 128), 128)
                        partial[c, at : at + GROUP, v] = value
            return 0

        lax.fori_loop(0, cols // COLS_STEP, columns, 0, unroll=UNROLL)

    if partial is not None:
        return

    @pl.when(step == pl.num_programs(0) - 1)
    def _():
        wide = len(sends) if len(sends) > 1 else sends[0].shape[0]
        count = sends[0].shape[-2]

        def store(out, to):
            for channel in range(4):
                for column in range(cols // 128):
                    value = acc_s[channel, column, pl.ds(to, count, wide), :]
                    out[channel, :, 128 * column : 128 * (column + 1)] = encode(value)

        if len(sends) > 1:
            me = lax.axis_index("wide")
            for k, out in enumerate(sends):
                store(out, jnp.bitwise_xor(me, k))
        else:
            lax.fori_loop(0, wide, lambda to, _: store(sends[0].at[to], to) or 0, 0)


def finish_kernel(parts, spots, *refs):
    image, codes, result, sems = refs[-4:]
    if parts > 1:
        me = lax.axis_index("wide")
        copies = [
            pltpu.make_async_copy(refs[k], codes.at[jnp.bitwise_xor(me, k)], sems.at[k])
            for k in range(parts)
        ]
    else:
        copies = [pltpu.make_async_copy(refs[0], codes, sems.at[0])]
    for copy in copies:
        copy.start()
    for copy in copies:
        copy.wait()
    wide, _, count, cols = codes.shape

    def columns(column, _):
        w = pl.ds(pl.multiple_of(128 * column, 128), 128)
        total = jnp.zeros((count, 128), jnp.float32)
        color = [total] * 3
        trans = jnp.ones_like(total)
        for source in range(wide):
            color = [color[c] + trans * decode(codes[source, c, :, w]) for c in range(3)]
            total = total - decode(codes[source, 3, :, w])
            trans = jnp.exp2(total)
        for c in range(3):
            result[:, c, w] = color[c]
        result[:, 3, w] = 1.0 - trans
        return 0

    lax.fori_loop(0, cols // 128, columns, 0, unroll=2)
    share = count // len(spots)
    copies = [
        pltpu.make_async_copy(
            result.at[i * share : (i + 1) * share], image.at[spot : spot + share], sems.at[i]
        )
        for i, spot in enumerate(spots)
    ]
    for copy in copies:
        copy.start()
    for copy in copies:
        copy.wait()


def split_rows(rows, wide):
    ends = max(ROW_BLOCK, wide)
    if wide > PERMUTES:
        return [[(ends, rows - ends)], [(0, ends), (rows - ends, rows)]]
    low, high = rows // 2 - ROW_BLOCK, rows // 2 + ROW_BLOCK
    return [
        [(low, high)],
        [(ends, low), (high, rows - ends)],
        [(0, ends), (rows - ends, rows)],
    ]


def shade(mode, ranges, wide, mass, heat, tables, edges=(), halo=(), inner=(), single=False):
    depth, rows, cols = mass.shape
    bumps = tables[1].shape[1]
    block = ROW_BLOCK
    ends = max(ROW_BLOCK, wide)
    size = sum(stop - start for start, stop in ranges)
    steps = size // block
    per8 = block // 8
    first = (ranges[0][1] - ranges[0][0]) // block
    lines = [line for start, stop in ranges for line in range(start, stop, GROUP)]

    def spot(i):
        if len(ranges) == 1:
            return i + ranges[0][0] // block
        return jnp.where(i < first, i + ranges[0][0] // block, i - first + ranges[1][0] // block)

    in_specs = [
        pl.BlockSpec((depth, block, cols), lambda i: (0, spot(i), 0)),
        pl.BlockSpec((depth, 8, cols), lambda i: (0, jnp.maximum(spot(i) * per8 - 1, 0), 0)),
        pl.BlockSpec(
            (depth, 8, cols),
            lambda i: (0, jnp.minimum((spot(i) + 1) * per8, rows // 8 - 1), 0),
        ),
        pl.BlockSpec((depth, block, cols), lambda i: (0, spot(i), 0)),
        *[pl.BlockSpec(value.shape, lambda i: (0, 0)) for value in tables],
    ]
    for _ in edges:
        in_specs.append(pl.BlockSpec((depth, 8, cols), lambda i: (0, 0, 0)))
    for _ in halo:
        in_specs.append(pl.BlockSpec((1, block, cols), lambda i: (0, spot(i), 0)))
    for _ in inner:
        in_specs.append(pl.BlockSpec((4, block, cols), lambda i: (0, spot(i) - ends // block, 0)))
    scratch = [
        pltpu.VMEM((block // GROUP, depth, GROUP * (bumps + 4), WIDTH), jnp.bfloat16),
        pltpu.VMEM((tables[1].shape[0], 16, WIDTH), jnp.float32),
        pltpu.VMEM((size // GROUP, depth, 128), jnp.int32),
    ]
    if mode == "inner":
        out_specs = pl.BlockSpec((4, block, cols), lambda i: (0, i, 0))
        out_shape = jax.ShapeDtypeStruct((4, size, cols), jnp.float32)
    else:
        shape = (4, size // wide, cols)
        if single:
            out_specs = [pl.BlockSpec((wide, *shape), lambda i: (0, 0, 0, 0))]
            out_shape = [jax.ShapeDtypeStruct((wide, *shape), jnp.int16)]
        else:
            out_specs = [pl.BlockSpec(shape, lambda i: (0, 0, 0))] * wide
            out_shape = [jax.ShapeDtypeStruct(shape, jnp.int16)] * wide
        scratch.append(pltpu.VMEM((4, cols // 128, size, 128), jnp.float32))
    layers = {"full": depth, "inner": depth - 2, "outer": 2}[mode]
    cells = size * cols * layers
    return pl.pallas_call(
        functools.partial(shade_kernel, mode, bool(edges), lines),
        grid=(steps,),
        in_specs=in_specs,
        out_specs=out_specs,
        out_shape=out_shape,
        scratch_shapes=scratch,
        compiler_params=pltpu.CompilerParams(vmem_limit_bytes=VMEM_BYTES),
        cost_estimate=pl.CostEstimate(
            flops=cells * 90, bytes_accessed=cells * 6, transcendentals=cells * 13
        ),
    )(mass, mass, mass, heat, *tables, *edges, *halo, *inner)


def finish(ranges, rows, wide, codes, image):
    count, cols = codes[0].shape[-2:]
    args, alias = [*codes], {}
    if image is not None:
        alias = {len(args): 0}
        args.append(image)
    spots = [start // wide for start, _ in ranges]
    cells = count * wide * cols
    return pl.pallas_call(
        functools.partial(finish_kernel, len(codes), spots),
        in_specs=[pl.BlockSpec(memory_space=pl.ANY)] * len(args),
        out_specs=pl.BlockSpec(memory_space=pl.ANY),
        out_shape=jax.ShapeDtypeStruct((rows // wide, 4, cols), jnp.float32),
        scratch_shapes=[
            pltpu.VMEM((wide, 4, count, cols), jnp.int16),
            pltpu.VMEM((count, 4, cols), jnp.float32),
            pltpu.SemaphoreType.DMA((max(len(codes), 2),)),
        ],
        input_output_aliases=alias,
        name="finish",
        compiler_params=pltpu.CompilerParams(vmem_limit_bytes=VMEM_BYTES),
        cost_estimate=pl.CostEstimate(
            flops=cells * 40, bytes_accessed=cells * 8, transcendentals=cells * 5
        ),
    )(*args)


def exchange(sends):
    if len(sends) == 1:
        return [lax.all_to_all(sends[0], "wide", 0, 0, tiled=True)]
    wide = len(sends)
    received = [*sends]
    for k in reversed(range(1, wide)):
        received[k] = lax.ppermute(sends[k], "wide", [(i, i ^ k) for i in range(wide)])
    return received


def per_device(mass, heat, picks, means, widths, heights, tint):
    depth, rows, cols = mass.shape
    wide = lax.axis_size("wide")

    def swap(value, axis, step):
        count = lax.axis_size(axis)
        pairs = [(i, i + step) for i in range(count) if 0 <= i + step < count]
        return lax.ppermute(value, axis, pairs)

    halo = (swap(mass[depth - 1 :], "wide", 1), swap(mass[:1], "wide", -1))
    parts = split_rows(rows, wide)
    tables = (picks, means, widths, heights, tint)
    ends = max(ROW_BLOCK, wide)
    inner = shade("inner", [(ends, rows - ends)], wide, mass, heat, tables)
    inner, later = lax.optimization_barrier((inner, mass))
    edges = (swap(later[:, rows - 8 :, :], "narrow", 1), swap(later[:, :8, :], "narrow", -1))

    sends = []
    for part, ranges in enumerate(parts):
        if part:
            means, *sends[-1] = lax.optimization_barrier((means, *sends[-1]))
        tables = (picks, means, widths, heights, tint)
        single = part == 0 or wide > PERMUTES
        if part < len(parts) - 1:
            send = shade(
                "outer", ranges, wide, mass, heat, tables, (), halo, (inner,), single
            )
        else:
            send = shade("full", ranges, wide, mass, heat, tables, edges, halo, (), single)
        sends.append(send)
    image = None
    for part, ranges in enumerate(parts):
        image = finish(ranges, rows, wide, exchange(sends[part]), image)
    return image.reshape(1, rows // wide, 1, 4, cols)


def solution(mesh):
    return jax.shard_map(
        per_device,
        mesh=mesh,
        in_specs=(
            P("wide", "narrow", None),
            P("wide", "narrow", None),
            P("wide", "narrow"),
            P(),
            P(),
            P(),
            P(),
        ),
        out_specs=P("narrow", None, "wide", None, None),
        check_vma=False,
    )
```
